32 devices in a mesh: chain: 2 (over x), slab: 16 (over z, y, core).
Axes of the slice: x: 2, y: 2, z: 4, core: 2. Of those that a mesh axis runs over, the one named last changes fastest.
Arguments:
- whitened: float32 [1024, 256, 256], P(('chain', 'slab')), parts along dimension 0, may hold values from -6 to 6
- counts: int32 [1024, 256, 256], P(('chain', 'slab')), parts along dimension 0, may hold values from 0 to 24
- exposure: int32 [1024, 256, 256], P(('chain', 'slab')), parts along dimension 0, may hold values from 1 to 12
- cholesky_east: float32 [512, 512], replicated, as said below
- cholesky_north: float32 [256, 256], replicated, as said below
- cholesky_time: float32 [256, 256], replicated, as said below
Outputs:
- gradient: float32 [1024, 256, 256], P(('chain', 'slab')), parts along dimension 0
- density: float32 [2], P('chain'), parts along dimension 0
The draws below stay inside these ranges and needn't reach their ends.
There are 2 independent parts, one for each index of `chain`. The reference program is written for one: setup_inputs(seed, part) draws one part's arguments, and reference() takes and returns one part's arrays. A program takes and returns all parts, laid end to end along the dimension named above; an argument that names none is the same for every part. Nothing has to cross between parts.
Inputs may be any that keep to these rules, and one draw needn't show every extreme that they name: `cholesky_east`: lower triangular with a positive diagonal, each row of unit length. `cholesky_north`: lower triangular with a positive diagonal, each row of unit length. `cholesky_time`: lower triangular with a positive diagonal, each row of unit length.
All inputs are finite; a program needn't handle non-finite values.
Results may differ from the reference program's by a relative error of at most 0.00008.
Values sent between devices are 32-bit elements; how exact they have to be, the bound alone decides.
A program may use at most 128 MiB of HBM per device.

```python
import jax
import jax.numpy as jnp
from jax import lax

NX = 512
NY = 256
NT = 256


def lower_factor(key, extent):
    key_off, key_diag = jax.random.split(key)
    random_part = jax.random.normal(key_off, (extent, extent), jnp.float32)
    row_index = lax.broadcasted_iota(jnp.int32, (extent, extent), 0)
    col_index = lax.broadcasted_iota(jnp.int32, (extent, extent), 1)
    spread = 0.6
    lower_part = jnp.where(col_index < row_index, random_part * spread / jnp.sqrt(row_index.astype(jnp.float32) + 1.0), 0.0)
    diagonal = jax.random.uniform(key_diag, (extent,), jnp.float32, 0.7, 1.3)
    lower_part = lower_part + jnp.diag(diagonal)
    return lower_part / jnp.sqrt(jnp.sum(lower_part * lower_part, axis=1, keepdims=True))


def draw_cholesky_east(key, part):
    return lower_factor(jax.random.fold_in(key, 101), NX)


def draw_cholesky_north(key, part):
    return lower_factor(jax.random.fold_in(key, 202), NY)


def draw_cholesky_time(key, part):
    return lower_factor(jax.random.fold_in(key, 303), NT)


def observed_pair(key):
    base_key = jax.random.fold_in(key, 404)
    key_exposure, key_counts = jax.random.split(base_key)
    east_index = lax.broadcasted_iota(jnp.int32, (NX, NY, NT), 0)
    exposure = jax.random.randint(key_exposure, (NX, NY, NT), 1, 5, dtype=jnp.int32) + 8 * east_index // NX
    counts = jax.random.randint(key_counts, (NX, NY, NT), 0, 2 * exposure + 1, dtype=jnp.int32)
    return (counts, exposure)


def draw_counts(key, part):
    return observed_pair(key)[0]


def draw_exposure(key, part):
    return observed_pair(key)[1]


def block_scale(rng, shape, cuts, low, top_value):
    level, own = 1.0, jax.random.fold_in(rng, 6)
    for axis_at, shards_of in cuts:
        draws = jnp.exp(jax.random.uniform(jax.random.fold_in(own, axis_at), (shards_of,), jnp.float32, low / len(cuts), top_value / len(cuts)))
        level = level * jnp.repeat(draws, shape[axis_at] // shards_of).reshape([-1 if axis == axis_at else 1 for axis in range(len(shape))])
    return level


def bell_draw(stream_key, dims, scale, limit, pieces=(), held_as=jnp.bfloat16):
    loudness = block_scale(stream_key, dims, pieces, -0.22, 0.18) if pieces else 1.0
    entries = jax.random.normal(stream_key, dims, jnp.float32) * scale * loudness
    return jnp.minimum(jnp.maximum(entries, -limit), limit).astype(held_as)


def setup_inputs(seed: int = 0, part: int = 0) -> dict:
    key_of = jax.random.split(jax.random.key(seed), 7)
    own_keys = jax.random.split(jax.random.fold_in(key_of[6], part), 7)
    whitened = bell_draw(own_keys[0], (NX, NY, NT), 1.0, 6.0, ((0, 16),), jnp.float32)
    counts = draw_counts(jax.random.fold_in(jax.random.fold_in(key_of[6], part), 71), part)
    exposure = draw_exposure(jax.random.fold_in(jax.random.fold_in(key_of[6], part), 71), part)
    cholesky_east = draw_cholesky_east(jax.random.fold_in(key_of[6], 71), part)
    cholesky_north = draw_cholesky_north(jax.random.fold_in(key_of[6], 71), part)
    cholesky_time = draw_cholesky_time(jax.random.fold_in(key_of[6], 71), part)
    return dict(whitened=whitened, counts=counts, exposure=exposure, cholesky_east=cholesky_east, cholesky_north=cholesky_north, cholesky_time=cholesky_time)


field_scale = 0.6


def mode_last(values, matrix):
    return jnp.einsum("abc,tc->abt", values, matrix, precision=lax.Precision.HIGHEST)


def mode_middle(values, matrix):
    return jnp.einsum("abc,yb->ayc", values, matrix, precision=lax.Precision.HIGHEST)


def mode_first(values, matrix):
    return jnp.einsum("abc,xa->xbc", values, matrix, precision=lax.Precision.HIGHEST)


def adjoint_last(values, matrix):
    return jnp.einsum("abt,tc->abc", values, matrix, precision=lax.Precision.HIGHEST)


def adjoint_middle(values, matrix):
    return jnp.einsum("ayc,yb->abc", values, matrix, precision=lax.Precision.HIGHEST)


def adjoint_first(values, matrix):
    return jnp.einsum("xbc,xa->abc", values, matrix, precision=lax.Precision.HIGHEST)


def reference(whitened, counts, exposure, cholesky_east, cholesky_north, cholesky_time):
    values = mode_first(mode_middle(mode_last(whitened, cholesky_time), cholesky_north), cholesky_east)
    log_rate = field_scale * values
    observed = counts.astype(jnp.float32)
    intensity = exposure.astype(jnp.float32) * jnp.exp(log_rate)
    residual = observed - intensity
    total_sum = jnp.sum(observed * log_rate - intensity) - 0.5 * jnp.sum(whitened * whitened)
    density = total_sum / (NX * NY * NT)
    adjoint = adjoint_last(adjoint_middle(adjoint_first(residual, cholesky_east), cholesky_north), cholesky_time)
    gradient = field_scale * adjoint - whitened
    return gradient, jnp.reshape(density, (1,))
```

```python
import functools

import jax
import jax.numpy as jnp
from jax import lax
from jax.experimental import pallas as pl
from jax.experimental.pallas import tpu as pltpu
from jax.sharding import PartitionSpec as P

field_scale = 0.6
QUARTERS = 4
MAX_CHUNKS = 16
AHEAD = 3
VMEM_BYTES = 67043328
HIGH = lax.Precision.HIGH


def split(values):
    high = values.astype(jnp.bfloat16)
    low = (values - high.astype(jnp.float32)).astype(jnp.bfloat16)
    return high, low


def dot(left, right):
    return jnp.dot(left, right, preferred_element_type=jnp.float32)


def kernel(
    group, chunks, q_hbm, cnt_hbm, exp_hbm, lh, ll, th, tl, out_hbm, acc,
    own, f0, f1, res, wgt, b0, b1,
    send_in, recv_p, recv_c, recv_e, send_z, recv_f0, recv_f1, recv_b0, recv_b1, send_g, recv_g,
):
    slab = lax.axis_index("slab")
    quarter = slab // group
    place = slab % group
    lines = own.shape[0]
    rows = own.shape[1]
    planes = q_hbm.shape[1]
    step = lines // chunks

    def device(quarter_of, place_of):
        return {"slab": quarter_of * group + place_of}

    barrier = pltpu.get_barrier_semaphore()
    for j in range(1, group):
        pl.semaphore_signal(barrier, inc=1, device_id=device(quarter, lax.rem(place + j, group)), device_id_type=pl.DeviceIdType.MESH)
    for j in range(1, QUARTERS):
        pl.semaphore_signal(barrier, inc=1, device_id=device(lax.rem(quarter + j, QUARTERS), place), device_id_type=pl.DeviceIdType.MESH)
    pl.semaphore_wait(barrier, group + QUARTERS - 2)

    acc[...] = jnp.zeros_like(acc)

    def part(chunk):
        return pl.ds(chunk * step, step)

    def remote(src, dst, send_sem, recv_sem, target):
        pltpu.make_async_remote_copy(
            src_ref=src, dst_ref=dst, send_sem=send_sem, recv_sem=recv_sem,
            device_id=target, device_id_type=pl.DeviceIdType.MESH,
        ).start()

    def await_bytes(ref, sem):
        pltpu.make_async_copy(ref, ref, sem).wait()

    def spread(chunk):
        mine = pl.ds(place * planes, planes)
        for k, (src, dst, recv) in enumerate(((q_hbm, own, recv_p), (cnt_hbm, res, recv_c), (exp_hbm, wgt, recv_e))):
            for j in range(1, group):
                to = lax.rem(place + j, group)
                remote(
                    src.at[pl.ds(to * lines + chunk * step, step)], dst.at[part(chunk), mine],
                    send_in.at[k], recv.at[chunk], device(quarter, to),
                )
            pltpu.make_async_copy(
                src.at[pl.ds(place * lines + chunk * step, step)], dst.at[part(chunk), mine], recv.at[chunk]
            ).start()

    def collect(chunk):
        for j in range(1, group):
            to = lax.rem(place + j, group)
            remote(
                wgt.at[part(chunk), pl.ds(to * planes, planes)],
                out_hbm.at[pl.ds(place * lines + chunk * step, step)],
                send_g, recv_g, device(quarter, to),
            )
        pltpu.make_async_copy(
            wgt.at[part(chunk), pl.ds(place * planes, planes)],
            out_hbm.at[pl.ds(place * lines + chunk * step, step)], recv_g,
        ).start()

    def product(high, low, row, terms, y, base=None):
        total = base
        for col, (x_high, x_low) in terms:
            block = (slice(row * rows, (row + 1) * rows), slice(col * rows, (col + 1) * rows))
            a_high, a_low = high[block], low[block]
            value = dot(a_high, x_high) + (dot(a_high, x_low) + dot(a_low, x_high))
            total = value if total is None else total + value
        return total

    def observe(y, field):
        log_rate = field_scale * field
        observed = res[y]
        intensity = wgt[y] * jnp.exp(log_rate)
        acc[...] += observed * log_rate - intensity
        res[y] = observed - intensity

    def over_lines(chunk, body):
        def at_line(i, carry):
            body(chunk * step + i)
            return carry

        lax.fori_loop(0, step, at_line, 0, unroll=min(step, 2))

    def forward(q, chunk):
        await_bytes(res.at[part(chunk)], recv_c.at[chunk])
        await_bytes(wgt.at[part(chunk)], recv_e.at[chunk])
        if q >= 1:
            await_bytes(f0.at[part(chunk)], recv_f0.at[chunk])
        if q == 2:
            await_bytes(f1.at[part(chunk)], recv_f1.at[chunk])

        def line(y):
            terms = [(q, split(own[y]))]
            if q in (1, 2):
                terms.append((q - 1, split(f0[y])))
            if q == 2:
                terms.append((0, split(f1[y])))
            observe(y, product(lh, ll, q, terms, y, f0[y] if q == 3 else None))
            if q == 2:
                b1[y] = product(lh, ll, 3, terms, y)

        over_lines(chunk, line)
        if q == 2:
            remote(b1.at[part(chunk)], f0.at[part(chunk)], send_z.at[0], recv_f0.at[chunk], device(3, place))
            remote(res.at[part(chunk)], b0.at[part(chunk)], send_z.at[1], recv_b0.at[chunk], device(1, place))
        if q == 3:
            remote(res.at[part(chunk)], b0.at[part(chunk)], send_z.at[0], recv_b0.at[chunk], device(2, place))
            remote(res.at[part(chunk)], b1.at[part(chunk)], send_z.at[1], recv_b1.at[chunk], device(1, place))

    def backward(q, chunk):
        if q <= 2:
            await_bytes(b0.at[part(chunk)], recv_b0.at[chunk])
        if q == 1:
            await_bytes(b1.at[part(chunk)], recv_b1.at[chunk])

        def line(y):
            terms = [(q, split(res[y]))]
            if q in (1, 2):
                terms.append((q + 1, split(b0[y])))
            if q == 1:
                terms.append((3, split(b1[y])))
            wgt[y] = product(th, tl, q, terms, y, b0[y] if q == 0 else None)
            if q == 1:
                f1[y] = product(th, tl, 0, terms, y)

        over_lines(chunk, line)
        if q == 1:
            remote(f1.at[part(chunk)], b0.at[part(chunk)], send_z.at[1], recv_b0.at[chunk], device(0, place))

    def onward(q, chunk):
        await_bytes(own.at[part(chunk)], recv_p.at[chunk])
        if q == 0:
            remote(own.at[part(chunk)], f0.at[part(chunk)], send_z.at[0], recv_f0.at[chunk], device(1, place))
            remote(own.at[part(chunk)], f1.at[part(chunk)], send_z.at[1], recv_f1.at[chunk], device(2, place))
        if q == 1:
            remote(own.at[part(chunk)], f0.at[part(chunk)], send_z.at[0], recv_f0.at[chunk], device(2, place))

    ahead = min(AHEAD, chunks)
    for chunk in range(ahead):
        spread(chunk)

    forward_lag = (1, 1, 1, 2)
    backward_lag = (4, 3, 3, 2)

    def turn(i, carry):
        @pl.when(i + ahead < chunks)
        def _():
            spread(i + ahead)

        for q in range(QUARTERS):
            @pl.when((quarter == q) & (i < chunks))
            def _(q=q):
                onward(q, i)

            @pl.when((quarter == q) & (i >= forward_lag[q]) & (i < chunks + forward_lag[q]))
            def _(q=q):
                forward(q, i - forward_lag[q])

            @pl.when((quarter == q) & (i >= backward_lag[q]) & (i < chunks + backward_lag[q]))
            def _(q=q):
                backward(q, i - backward_lag[q])
                collect(i - backward_lag[q])

        return carry

    lax.fori_loop(0, chunks + max(backward_lag), turn, 0)

    away = pl.ds(0, (group - 1) * lines)
    if group > 1:
        for k, src in enumerate((q_hbm, cnt_hbm, exp_hbm)):
            await_bytes(src.at[away], send_in.at[k])
        await_bytes(out_hbm.at[away], send_g)
    for k in range(2):
        await_bytes(own, send_z.at[k])
    await_bytes(out_hbm, recv_g)


def exchange(partly, counts, exposure, east, group):
    lines = partly.shape[0] // group
    rows = partly.shape[1] * group
    times = partly.shape[2]
    chunks = min(MAX_CHUNKS, lines)
    rounded = lax.reduce_precision(east, 8, 7)
    high, low = rounded.astype(jnp.bfloat16), (east - rounded).astype(jnp.bfloat16)
    whole = lambda: pltpu.VMEM((lines, rows, times), jnp.float32)
    any_space = pl.BlockSpec(memory_space=pl.ANY)
    in_vmem = pl.BlockSpec(memory_space=pltpu.VMEM)
    dma = pltpu.SemaphoreType.DMA
    return pl.pallas_call(
        functools.partial(kernel, group, chunks),
        out_shape=(
            jax.ShapeDtypeStruct(partly.shape, jnp.float32),
            jax.ShapeDtypeStruct((rows, times), jnp.float32),
        ),
        in_specs=[any_space] * 3 + [in_vmem] * 4,
        out_specs=(any_space, in_vmem),
        scratch_shapes=[whole() for _ in range(7)]
        + [dma((3,))]
        + [dma((chunks,)) for _ in range(3)]
        + [dma((2,))]
        + [dma((chunks,)) for _ in range(4)]
        + [dma, dma],
        compiler_params=pltpu.CompilerParams(
            collective_id=0, has_side_effects=True, vmem_limit_bytes=VMEM_BYTES
        ),
    )(partly, counts, exposure, high, low, high.T, low.T)


def per_device(whitened, counts, exposure, cholesky_east, cholesky_north, cholesky_time):
    slabs = lax.axis_size("slab")
    cell_count = whitened.shape[0] * whitened.shape[1] * whitened.shape[2]
    prior_term = -0.5 * jnp.sum(whitened * whitened)
    partly = jnp.einsum("abc,tc->abt", whitened, cholesky_time, precision=HIGH)
    partly = jnp.einsum("abt,yb->yat", partly, cholesky_north, precision=HIGH)
    counts_lines = jnp.transpose(counts.astype(jnp.float32), (1, 0, 2))
    exposure_lines = jnp.transpose(exposure.astype(jnp.float32), (1, 0, 2))
    adjoint, terms = exchange(partly, counts_lines, exposure_lines, cholesky_east, slabs // QUARTERS)
    adjoint = jnp.einsum("yat,yb->abt", adjoint, cholesky_north, precision=HIGH)
    adjoint = jnp.einsum("abt,tc->abc", adjoint, cholesky_time, precision=HIGH)
    gradient = field_scale * adjoint - whitened
    total_sum = lax.psum(jnp.sum(terms) + prior_term, "slab")
    density = total_sum / (cell_count * slabs)
    return (gradient, jnp.reshape(density, (1,)))


def solution(mesh):
    placed = (
        P(("chain", "slab"), None, None),
        P(("chain", "slab"), None, None),
        P(("chain", "slab"), None, None),
        P(),
        P(),
        P(),
    )
    return jax.shard_map(
        per_device,
        mesh=mesh,
        in_specs=placed,
        out_specs=(P(("chain", "slab"), None, None), P("chain")),
        check_vma=False,
    )
```

```python
import functools

import jax
import jax.numpy as jnp
from jax import lax
from jax.experimental import pallas as pl
from jax.experimental.pallas import tpu as pltpu
from jax.sharding import PartitionSpec as P

field_scale = 0.6
QUARTERS = 4
MAX_CHUNKS = 32
AHEAD = 6
VMEM_BYTES = 67043328
HIGH = lax.Precision.HIGH


def split(values):
    high = values.astype(jnp.bfloat16)
    low = (values - high.astype(jnp.float32)).astype(jnp.bfloat16)
    return high, low


def dot(left, right):
    return jnp.dot(left, right, preferred_element_type=jnp.float32)


def kernel(
    group, chunks, q_hbm, cnt_hbm, exp_hbm, w_hbm, lh, ll, th, tl, out_hbm, density,
    own, f0, f1, res, wgt, b0, b1, acc, prior, held, near, far,
    send_in, recv_p, recv_c, recv_e, send_z, recv_f0, recv_f1, recv_b0, recv_b1, send_g, recv_g,
    held_sem, send_near, recv_near, send_far, recv_far,
):
    slab = lax.axis_index("slab")
    quarter = slab // group
    place = slab % group
    lines = own.shape[0]
    rows = own.shape[1]
    planes = q_hbm.shape[1]
    step = lines // chunks

    def device(quarter_of, place_of):
        return {"slab": quarter_of * group + place_of}

    barrier = pltpu.get_barrier_semaphore()
    for j in range(1, group):
        pl.semaphore_signal(barrier, inc=1, device_id=device(quarter, lax.rem(place + j, group)), device_id_type=pl.DeviceIdType.MESH)
    for j in range(1, QUARTERS):
        pl.semaphore_signal(barrier, inc=1, device_id=device(lax.rem(quarter + j, QUARTERS), place), device_id_type=pl.DeviceIdType.MESH)
    pl.semaphore_wait(barrier, group + QUARTERS - 2)

    acc[...] = jnp.zeros_like(acc)
    prior[...] = jnp.zeros_like(prior)
    depth = held.shape[0]
    lanes = density.shape[1]

    def part(chunk):
        return pl.ds(chunk * step, step)

    def remote(src, dst, send_sem, recv_sem, target):
        pltpu.make_async_remote_copy(
            src_ref=src, dst_ref=dst, send_sem=send_sem, recv_sem=recv_sem,
            device_id=target, device_id_type=pl.DeviceIdType.MESH,
        ).start()

    def await_bytes(ref, sem):
        pltpu.make_async_copy(ref, ref, sem).wait()

    def spread(chunk):
        mine = pl.ds(place * planes, planes)
        for k, (src, dst, recv) in enumerate(((q_hbm, own, recv_p), (cnt_hbm, res, recv_c), (exp_hbm, wgt, recv_e))):
            for j in range(1, group):
                to = lax.rem(place + j, group)
                remote(
                    src.at[pl.ds(to * lines + chunk * step, step)], dst.at[part(chunk), mine],
                    send_in.at[k], recv.at[chunk], device(quarter, to),
                )
            pltpu.make_async_copy(
                src.at[pl.ds(place * lines + chunk * step, step)], dst.at[part(chunk), mine], recv.at[chunk]
            ).start()

    def collect(chunk):
        for j in range(1, group):
            to = lax.rem(place + j, group)
            remote(
                wgt.at[part(chunk), pl.ds(to * planes, planes)],
                out_hbm.at[pl.ds(place * lines + chunk * step, step)],
                send_g, recv_g, device(quarter, to),
            )
        pltpu.make_async_copy(
            wgt.at[part(chunk), pl.ds(place * planes, planes)],
            out_hbm.at[pl.ds(place * lines + chunk * step, step)], recv_g,
        ).start()

    def product(high, low, row, terms, y, base=None):
        total = base
        for col, (x_high, x_low) in terms:
            block = (slice(row * rows, (row + 1) * rows), slice(col * rows, (col + 1) * rows))
            a_high, a_low = high[block], low[block]
            value = dot(a_high, x_high) + (dot(a_high, x_low) + dot(a_low, x_high))
            total = value if total is None else total + value
        return total

    def observe(y, field):
        log_rate = field_scale * field
        observed = res[y]
        intensity = wgt[y] * jnp.exp(log_rate)
        acc[...] += observed * log_rate - intensity
        res[y] = observed - intensity

    def over_lines(chunk, body):
        def at_line(i, carry):
            body(chunk * step + i)
            return carry

        lax.fori_loop(0, step, at_line, 0, unroll=min(step, 2))

    def forward(q, chunk):
        await_bytes(res.at[part(chunk)], recv_c.at[chunk])
        await_bytes(wgt.at[part(chunk)], recv_e.at[chunk])
        if q >= 1:
            await_bytes(f0.at[part(chunk)], recv_f0.at[chunk])
        if q == 2:
            await_bytes(f1.at[part(chunk)], recv_f1.at[chunk])

        def line(y):
            terms = [(q, split(own[y]))]
            if q in (1, 2):
                terms.append((q - 1, split(f0[y])))
            if q == 2:
                terms.append((0, split(f1[y])))
            observe(y, product(lh, ll, q, terms, y, f0[y] if q == 3 else None))
            if q == 2:
                b1[y] = product(lh, ll, 3, terms, y)

        over_lines(chunk, line)
        if q == 2:
            remote(b1.at[part(chunk)], f0.at[part(chunk)], send_z.at[0], recv_f0.at[chunk], device(3, place))
            remote(res.at[part(chunk)], b0.at[part(chunk)], send_z.at[1], recv_b0.at[chunk], device(1, place))
        if q == 3:
            remote(res.at[part(chunk)], b0.at[part(chunk)], send_z.at[0], recv_b0.at[chunk], device(2, place))
            remote(res.at[part(chunk)], b1.at[part(chunk)], send_z.at[1], recv_b1.at[chunk], device(1, place))

    def backward(q, chunk):
        if q <= 2:
            await_bytes(b0.at[part(chunk)], recv_b0.at[chunk])
        if q == 1:
            await_bytes(b1.at[part(chunk)], recv_b1.at[chunk])

        def line(y):
            terms = [(q, split(res[y]))]
            if q in (1, 2):
                terms.append((q + 1, split(b0[y])))
            if q == 1:
                terms.append((3, split(b1[y])))
            wgt[y] = product(th, tl, q, terms, y, b0[y] if q == 0 else None)
            if q == 1:
                f1[y] = product(th, tl, 0, terms, y)

        over_lines(chunk, line)
        if q == 1:
            remote(f1.at[part(chunk)], b0.at[part(chunk)], send_z.at[1], recv_b0.at[chunk], device(0, place))

    def onward(q, chunk):
        await_bytes(own.at[part(chunk)], recv_p.at[chunk])
        if q == 0:
            remote(own.at[part(chunk)], f0.at[part(chunk)], send_z.at[0], recv_f0.at[chunk], device(1, place))
            remote(own.at[part(chunk)], f1.at[part(chunk)], send_z.at[1], recv_f1.at[chunk], device(2, place))
        if q == 1:
            remote(own.at[part(chunk)], f0.at[part(chunk)], send_z.at[0], recv_f0.at[chunk], device(2, place))

    def fetch(chunk):
        return pltpu.make_async_copy(w_hbm.at[pl.ds(chunk * depth, depth)], held, held_sem)

    def square():
        values = held[...]
        prior[...] += jnp.sum((values * values).reshape(depth // 8, 8, values.shape[1]), axis=0)

    def fold(tile):
        return sum(tile[:, k * lanes : (k + 1) * lanes] for k in range(tile.shape[1] // lanes))

    def send_sum_near():
        cells = jnp.sum(acc[...].reshape(rows // 8, 8, acc.shape[1]), axis=0)
        near[place] = fold(cells - 0.5 * prior[...])
        for j in range(1, group):
            remote(near.at[place], near.at[place], send_near, recv_near, device(quarter, lax.rem(place + j, group)))

    def send_sum_far():
        if group > 1:
            others = near.at[pl.ds(0, group - 1)]
            await_bytes(others, send_near)
            await_bytes(others, recv_near)
        far[quarter] = jnp.sum(near[...], axis=0)
        for j in range(1, QUARTERS):
            remote(far.at[quarter], far.at[quarter], send_far, recv_far, device(lax.rem(quarter + j, QUARTERS), place))

    ahead = min(AHEAD, chunks)
    for chunk in range(ahead):
        spread(chunk)

    forward_lag = (1, 1, 1, 2)
    backward_lag = (4, 3, 3, 2)

    def turn(i, carry):
        @pl.when(i < chunks)
        def _():
            fetch(i).start()

        @pl.when(i + ahead < chunks)
        def _():
            spread(i + ahead)

        for q in range(QUARTERS):
            @pl.when((quarter == q) & (i < chunks))
            def _(q=q):
                onward(q, i)

            @pl.when((quarter == q) & (i >= forward_lag[q]) & (i < chunks + forward_lag[q]))
            def _(q=q):
                forward(q, i - forward_lag[q])

            @pl.when((quarter == q) & (i >= backward_lag[q]) & (i < chunks + backward_lag[q]))
            def _(q=q):
                backward(q, i - backward_lag[q])
                collect(i - backward_lag[q])

        @pl.when(i < chunks)
        def _():
            fetch(i).wait()
            square()

        @pl.when(i == chunks + max(forward_lag) - 1)
        def _():
            send_sum_near()

        @pl.when(i == chunks + max(forward_lag))
        def _():
            send_sum_far()

        return carry

    lax.fori_loop(0, chunks + max(backward_lag), turn, 0)

    others = far.at[pl.ds(0, QUARTERS - 1)]
    await_bytes(others, send_far)
    await_bytes(others, recv_far)
    density[...] = jnp.sum(far[...], axis=0)

    away = pl.ds(0, (group - 1) * lines)
    if group > 1:
        for k, src in enumerate((q_hbm, cnt_hbm, exp_hbm)):
            await_bytes(src.at[away], send_in.at[k])
        await_bytes(out_hbm.at[away], send_g)
    for k in range(2):
        await_bytes(own, send_z.at[k])
    await_bytes(out_hbm, recv_g)


def exchange(partly, counts, exposure, whitened, east, group):
    lines = partly.shape[0] // group
    rows = partly.shape[1] * group
    times = partly.shape[2]
    chunks = min(MAX_CHUNKS, lines)
    rounded = lax.reduce_precision(east, 8, 7)
    high, low = rounded.astype(jnp.bfloat16), (east - rounded).astype(jnp.bfloat16)
    depth = whitened.shape[0] // chunks
    whole = lambda: pltpu.VMEM((lines, rows, times), jnp.float32)
    any_space = pl.BlockSpec(memory_space=pl.ANY)
    in_vmem = pl.BlockSpec(memory_space=pltpu.VMEM)
    dma = pltpu.SemaphoreType.DMA
    return pl.pallas_call(
        functools.partial(kernel, group, chunks),
        out_shape=(
            jax.ShapeDtypeStruct(partly.shape, jnp.float32),
            jax.ShapeDtypeStruct((8, 128), jnp.float32),
        ),
        in_specs=[any_space] * 4 + [in_vmem] * 4,
        out_specs=(any_space, in_vmem),
        scratch_shapes=[whole() for _ in range(7)]
        + [
            pltpu.VMEM((rows, times), jnp.float32),
            pltpu.VMEM((8, times), jnp.float32),
            pltpu.VMEM((depth, times), jnp.float32),
            pltpu.VMEM((group, 8, 128), jnp.float32),
            pltpu.VMEM((QUARTERS, 8, 128), jnp.float32),
        ]
        + [dma((3,))]
        + [dma((chunks,)) for _ in range(3)]
        + [dma((2,))]
        + [dma((chunks,)) for _ in range(4)]
        + [dma] * 7,
        compiler_params=pltpu.CompilerParams(
            collective_id=0, has_side_effects=True, vmem_limit_bytes=VMEM_BYTES
        ),
    )(partly, counts, exposure, whitened, high, low, high.T, low.T)


def per_device(whitened, counts, exposure, cholesky_east, cholesky_north, cholesky_time):
    slabs = lax.axis_size("slab")
    cell_count = whitened.shape[0] * whitened.shape[1] * whitened.shape[2]
    partly = jnp.einsum("abc,tc->abt", whitened, cholesky_time, precision=HIGH)
    partly = jnp.einsum("abt,yb->yat", partly, cholesky_north, precision=HIGH)
    counts_lines = jnp.transpose(counts.astype(jnp.float32), (1, 0, 2))
    exposure_lines = jnp.transpose(exposure.astype(jnp.float32), (1, 0, 2))
    flat = jnp.reshape(whitened, (-1, whitened.shape[2]))
    adjoint, terms = exchange(partly, counts_lines, exposure_lines, flat, cholesky_east, slabs // QUARTERS)
    adjoint = jnp.einsum("yat,yb->abt", adjoint, cholesky_north, precision=HIGH)
    adjoint = jnp.einsum("abt,tc->abc", adjoint, cholesky_time, precision=HIGH)
    gradient = field_scale * adjoint - whitened
    density = jnp.sum(terms) / (cell_count * slabs)
    return (gradient, jnp.reshape(density, (1,)))


def solution(mesh):
    placed = (
        P(("chain", "slab"), None, None),
        P(("chain", "slab"), None, None),
        P(("chain", "slab"), None, None),
        P(),
        P(),
        P(),
    )
    return jax.shard_map(
        per_device,
        mesh=mesh,
        in_specs=placed,
        out_specs=(P(("chain", "slab"), None, None), P("chain")),
        check_vma=False,
    )
```

```python
import functools

import jax
import jax.numpy as jnp
from jax import lax
from jax.experimental import pallas as pl
from jax.experimental.pallas import tpu as pltpu
from jax.sharding import PartitionSpec as P

field_scale = 0.6
QUARTERS = 4
MAX_CHUNKS = 64
AHEAD = 12
VMEM_BYTES = 67043328
HIGH = lax.Precision.HIGH


def split(values):
    high = values.astype(jnp.bfloat16)
    low = (values - high.astype(jnp.float32)).astype(jnp.bfloat16)
    return high, low


def dot(left, right):
    return jnp.dot(left, right, preferred_element_type=jnp.float32)


def kernel(
    group, chunks, q_hbm, cnt_hbm, exp_hbm, w_hbm, lh, ll, th, tl, out_hbm, density,
    own, f0, f1, res, wgt, b0, b1, acc, prior, held, near, far,
    send_in, recv_p, recv_c, recv_e, send_z, recv_f0, recv_f1, recv_b0, recv_b1, send_g, recv_g,
    held_sem, send_near, recv_near, send_far, recv_far,
):
    slab = lax.axis_index("slab")
    quarter = slab // group
    place = slab % group
    lines = own.shape[0]
    rows = own.shape[1]
    planes = q_hbm.shape[1]
    step = lines // chunks

    def device(quarter_of, place_of):
        return {"slab": quarter_of * group + place_of}

    barrier = pltpu.get_barrier_semaphore()
    for j in range(1, group):
        pl.semaphore_signal(barrier, inc=1, device_id=device(quarter, lax.rem(place + j, group)), device_id_type=pl.DeviceIdType.MESH)
    for j in range(1, QUARTERS):
        pl.semaphore_signal(barrier, inc=1, device_id=device(lax.rem(quarter + j, QUARTERS), place), device_id_type=pl.DeviceIdType.MESH)
    pl.semaphore_wait(barrier, group + QUARTERS - 2)

    acc[...] = jnp.zeros_like(acc)
    prior[...] = jnp.zeros_like(prior)
    depth = held.shape[0]
    lanes = density.shape[1]

    def part(chunk):
        return pl.ds(chunk * step, step)

    def remote(src, dst, send_sem, recv_sem, target):
        pltpu.make_async_remote_copy(
            src_ref=src, dst_ref=dst, send_sem=send_sem, recv_sem=recv_sem,
            device_id=target, device_id_type=pl.DeviceIdType.MESH,
        ).start()

    def await_bytes(ref, sem):
        pltpu.make_async_copy(ref, ref, sem).wait()

    def spread(chunk):
        mine = pl.ds(place * planes, planes)
        for k, (src, dst, recv) in enumerate(((q_hbm, own, recv_p), (cnt_hbm, res, recv_c), (exp_hbm, wgt, recv_e))):
            for j in range(1, group):
                to = lax.rem(place + j, group)
                remote(
                    src.at[pl.ds(to * lines + chunk * step, step)], dst.at[part(chunk), mine],
                    send_in.at[k], recv.at[chunk], device(quarter, to),
                )
            pltpu.make_async_copy(
                src.at[pl.ds(place * lines + chunk * step, step)], dst.at[part(chunk), mine], recv.at[chunk]
            ).start()

    def collect(chunk):
        for j in range(1, group):
            to = lax.rem(place + j, group)
            remote(
                wgt.at[part(chunk), pl.ds(to * planes, planes)],
                out_hbm.at[pl.ds(place * lines + chunk * step, step)],
                send_g, recv_g, device(quarter, to),
            )
        pltpu.make_async_copy(
            wgt.at[part(chunk), pl.ds(place * planes, planes)],
            out_hbm.at[pl.ds(place * lines + chunk * step, step)], recv_g,
        ).start()

    def product(high, low, row, terms, y, base=None):
        total = base
        for col, (x_high, x_low) in terms:
            block = (slice(row * rows, (row + 1) * rows), slice(col * rows, (col + 1) * rows))
            a_high, a_low = high[block], low[block]
            value = dot(a_high, x_high) + (dot(a_high, x_low) + dot(a_low, x_high))
            total = value if total is None else total + value
        return total

    def observe(y, field):
        log_rate = field_scale * field
        observed = res[y]
        intensity = wgt[y] * jnp.exp(log_rate)
        acc[...] += observed * log_rate - intensity
        res[y] = observed - intensity

    def over_lines(chunk, body):
        def at_line(i, carry):
            body(chunk * step + i)
            return carry

        lax.fori_loop(0, step, at_line, 0, unroll=min(step, 2))

    def forward(q, chunk):
        await_bytes(res.at[part(chunk)], recv_c.at[chunk])
        await_bytes(wgt.at[part(chunk)], recv_e.at[chunk])
        if q >= 1:
            await_bytes(f0.at[part(chunk)], recv_f0.at[chunk])
        if q == 2:
            await_bytes(f1.at[part(chunk)], recv_f1.at[chunk])

        def line(y):
            terms = [(q, split(own[y]))]
            if q in (1, 2):
                terms.append((q - 1, split(f0[y])))
            if q == 2:
                terms.append((0, split(f1[y])))
            observe(y, product(lh, ll, q, terms, y, f0[y] if q == 3 else None))
            if q == 2:
                b1[y] = product(lh, ll, 3, terms, y)

        over_lines(chunk, line)
        if q == 2:
            remote(b1.at[part(chunk)], f0.at[part(chunk)], send_z.at[0], recv_f0.at[chunk], device(3, place))
            remote(res.at[part(chunk)], b0.at[part(chunk)], send_z.at[1], recv_b0.at[chunk], device(1, place))
        if q == 3:
            remote(res.at[part(chunk)], b0.at[part(chunk)], send_z.at[0], recv_b0.at[chunk], device(2, place))
            remote(res.at[part(chunk)], b1.at[part(chunk)], send_z.at[1], recv_b1.at[chunk], device(1, place))

    def backward(q, chunk):
        if q <= 2:
            await_bytes(b0.at[part(chunk)], recv_b0.at[chunk])
        if q == 1:
            await_bytes(b1.at[part(chunk)], recv_b1.at[chunk])

        def line(y):
            terms = [(q, split(res[y]))]
            if q in (1, 2):
                terms.append((q + 1, split(b0[y])))
            if q == 1:
                terms.append((3, split(b1[y])))
            wgt[y] = product(th, tl, q, terms, y, b0[y] if q == 0 else None)
            if q == 1:
                f1[y] = product(th, tl, 0, terms, y)

        over_lines(chunk, line)
        if q == 1:
            remote(f1.at[part(chunk)], b0.at[part(chunk)], send_z.at[1], recv_b0.at[chunk], device(0, place))

    def onward(q, chunk):
        await_bytes(own.at[part(chunk)], recv_p.at[chunk])
        if q == 0:
            remote(own.at[part(chunk)], f0.at[part(chunk)], send_z.at[0], recv_f0.at[chunk], device(1, place))
            remote(own.at[part(chunk)], f1.at[part(chunk)], send_z.at[1], recv_f1.at[chunk], device(2, place))
        if q == 1:
            remote(own.at[part(chunk)], f0.at[part(chunk)], send_z.at[0], recv_f0.at[chunk], device(2, place))

    def fetch(chunk):
        return pltpu.make_async_copy(w_hbm.at[pl.ds(chunk * depth, depth)], held, held_sem)

    def square():
        values = held[...]
        prior[...] += jnp.sum((values * values).reshape(depth // 8, 8, values.shape[1]), axis=0)

    def fold(tile):
        return sum(tile[:, k * lanes : (k + 1) * lanes] for k in range(tile.shape[1] // lanes))

    def send_sum_near():
        cells = jnp.sum(acc[...].reshape(rows // 8, 8, acc.shape[1]), axis=0)
        near[place] = fold(cells - 0.5 * prior[...])
        for j in range(1, group):
            remote(near.at[place], near.at[place], send_near, recv_near, device(quarter, lax.rem(place + j, group)))

    def send_sum_far():
        if group > 1:
            others = near.at[pl.ds(0, group - 1)]
            await_bytes(others, send_near)
            await_bytes(others, recv_near)
        far[quarter] = jnp.sum(near[...], axis=0)
        for j in range(1, QUARTERS):
            remote(far.at[quarter], far.at[quarter], send_far, recv_far, device(lax.rem(quarter + j, QUARTERS), place))

    ahead = min(AHEAD, chunks)
    for chunk in range(ahead):
        spread(chunk)

    forward_lag = (1, 1, 1, 2)
    backward_lag = (4, 3, 3, 2)

    def turn(i, carry):
        @pl.when(i < chunks)
        def _():
            fetch(i).start()

        @pl.when(i + ahead < chunks)
        def _():
            spread(i + ahead)

        for q in range(QUARTERS):
            @pl.when((quarter == q) & (i < chunks))
            def _(q=q):
                onward(q, i)

            @pl.when((quarter == q) & (i >= forward_lag[q]) & (i < chunks + forward_lag[q]))
            def _(q=q):
                forward(q, i - forward_lag[q])

            @pl.when((quarter == q) & (i >= backward_lag[q]) & (i < chunks + backward_lag[q]))
            def _(q=q):
                backward(q, i - backward_lag[q])
                collect(i - backward_lag[q])

        @pl.when(i < chunks)
        def _():
            fetch(i).wait()
            square()

        @pl.when(i == chunks + max(forward_lag) - 1)
        def _():
            send_sum_near()

        @pl.when(i == chunks + max(forward_lag))
        def _():
            send_sum_far()

        return carry

    lax.fori_loop(0, chunks + max(backward_lag), turn, 0)

    others = far.at[pl.ds(0, QUARTERS - 1)]
    await_bytes(others, send_far)
    await_bytes(others, recv_far)
    density[...] = jnp.sum(far[...], axis=0)

    away = pl.ds(0, (group - 1) * lines)
    if group > 1:
        for k, src in enumerate((q_hbm, cnt_hbm, exp_hbm)):
            await_bytes(src.at[away], send_in.at[k])
        await_bytes(out_hbm.at[away], send_g)
    for k in range(2):
        await_bytes(own, send_z.at[k])
    await_bytes(out_hbm, recv_g)


def exchange(partly, counts, exposure, whitened, east, group):
    lines = partly.shape[0] // group
    rows = partly.shape[1] * group
    times = partly.shape[2]
    chunks = min(MAX_CHUNKS, lines)
    rounded = lax.reduce_precision(east, 8, 7)
    high, low = rounded.astype(jnp.bfloat16), (east - rounded).astype(jnp.bfloat16)
    depth = whitened.shape[0] // chunks
    whole = lambda: pltpu.VMEM((lines, rows, times), jnp.float32)
    any_space = pl.BlockSpec(memory_space=pl.ANY)
    in_vmem = pl.BlockSpec(memory_space=pltpu.VMEM)
    dma = pltpu.SemaphoreType.DMA
    return pl.pallas_call(
        functools.partial(kernel, group, chunks),
        out_shape=(
            jax.ShapeDtypeStruct(partly.shape, jnp.float32),
            jax.ShapeDtypeStruct((8, 128), jnp.float32),
        ),
        in_specs=[any_space] * 4 + [in_vmem] * 4,
        out_specs=(any_space, in_vmem),
        scratch_shapes=[whole() for _ in range(7)]
        + [
            pltpu.VMEM((rows, times), jnp.float32),
            pltpu.VMEM((8, times), jnp.float32),
            pltpu.VMEM((depth, times), jnp.float32),
            pltpu.VMEM((group, 8, 128), jnp.float32),
            pltpu.VMEM((QUARTERS, 8, 128), jnp.float32),
        ]
        + [dma((3,))]
        + [dma((chunks,)) for _ in range(3)]
        + [dma((2,))]
        + [dma((chunks,)) for _ in range(4)]
        + [dma] * 7,
        compiler_params=pltpu.CompilerParams(
            collective_id=0, has_side_effects=True, vmem_limit_bytes=VMEM_BYTES
        ),
    )(partly, counts, exposure, whitened, high, low, high.T, low.T)


def per_device(whitened, counts, exposure, cholesky_east, cholesky_north, cholesky_time):
    slabs = lax.axis_size("slab")
    cell_count = whitened.shape[0] * whitened.shape[1] * whitened.shape[2]
    partly = jnp.einsum("abc,tc->abt", whitened, cholesky_time, precision=HIGH)
    partly = jnp.einsum("abt,yb->yat", partly, cholesky_north, precision=HIGH)
    counts_lines = jnp.transpose(counts.astype(jnp.float32), (1, 0, 2))
    exposure_lines = jnp.transpose(exposure.astype(jnp.float32), (1, 0, 2))
    flat = jnp.reshape(whitened, (-1, whitened.shape[2]))
    adjoint, terms = exchange(partly, counts_lines, exposure_lines, flat, cholesky_east, slabs // QUARTERS)
    adjoint = jnp.einsum("yat,yb->abt", adjoint, cholesky_north, precision=HIGH)
    adjoint = jnp.einsum("abt,tc->abc", adjoint, cholesky_time, precision=HIGH)
    gradient = field_scale * adjoint - whitened
    density = jnp.sum(terms) / (cell_count * slabs)
    return (gradient, jnp.reshape(density, (1,)))


def solution(mesh):
    placed = (
        P(("chain", "slab"), None, None),
        P(("chain", "slab"), None, None),
        P(("chain", "slab"), None, None),
        P(),
        P(),
        P(),
    )
    return jax.shard_map(
        per_device,
        mesh=mesh,
        in_specs=placed,
        out_specs=(P(("chain", "slab"), None, None), P("chain")),
        check_vma=False,
    )
```

```python
import functools

import jax
import jax.numpy as jnp
from jax import lax
from jax.experimental import pallas as pl
from jax.experimental.pallas import tpu as pltpu
from jax.sharding import PartitionSpec as P

field_scale = 0.6
QUARTERS = 4
MAX_CHUNKS = 64
AHEAD = 12
VMEM_BYTES = 67043328
HIGH = lax.Precision.HIGH


def split(values):
    high = values.astype(jnp.bfloat16)
    low = (values - high.astype(jnp.float32)).astype(jnp.bfloat16)
    return high, low


def halves(matrix):
    rounded = lax.reduce_precision(matrix, 8, 7)
    return rounded.astype(jnp.bfloat16), (matrix - rounded).astype(jnp.bfloat16)


def dot(left, right):
    return jnp.dot(left, right, preferred_element_type=jnp.float32)


def kernel(
    group, chunks, q_hbm, cnt_hbm, exp_hbm, w_hbm, lh, ll, th, tl, out_hbm, density,
    own, f0, f1, res, wgt, b0, b1, acc, prior, held, near, far,
    send_in, recv_p, recv_c, recv_e, send_z, recv_f0, recv_f1, recv_b0, recv_b1, send_g, recv_g,
    held_sem, send_near, recv_near, send_far, recv_far,
):
    slab = lax.axis_index("slab")
    quarter = slab // group
    place = slab % group
    lines = own.shape[0]
    rows = own.shape[1]
    planes = q_hbm.shape[1]
    step = lines // chunks

    def device(quarter_of, place_of):
        return {"slab": quarter_of * group + place_of}

    barrier = pltpu.get_barrier_semaphore()
    for j in range(1, group):
        pl.semaphore_signal(barrier, inc=1, device_id=device(quarter, lax.rem(place + j, group)), device_id_type=pl.DeviceIdType.MESH)
    for j in range(1, QUARTERS):
        pl.semaphore_signal(barrier, inc=1, device_id=device(lax.rem(quarter + j, QUARTERS), place), device_id_type=pl.DeviceIdType.MESH)
    pl.semaphore_wait(barrier, group + QUARTERS - 2)

    acc[...] = jnp.zeros_like(acc)
    prior[...] = jnp.zeros_like(prior)
    depth = held.shape[0]
    lanes = density.shape[1]

    def part(chunk):
        return pl.ds(chunk * step, step)

    def remote(src, dst, send_sem, recv_sem, target):
        pltpu.make_async_remote_copy(
            src_ref=src, dst_ref=dst, send_sem=send_sem, recv_sem=recv_sem,
            device_id=target, device_id_type=pl.DeviceIdType.MESH,
        ).start()

    def await_bytes(ref, sem):
        pltpu.make_async_copy(ref, ref, sem).wait()

    def spread(chunk):
        mine = pl.ds(place * planes, planes)
        for k, (src, dst, recv) in enumerate(((q_hbm, own, recv_p), (cnt_hbm, res, recv_c), (exp_hbm, wgt, recv_e))):
            for j in range(1, group):
                to = lax.rem(place + j, group)
                remote(
                    src.at[pl.ds(to * lines + chunk * step, step)], dst.at[part(chunk), mine],
                    send_in.at[k], recv.at[chunk], device(quarter, to),
                )
            pltpu.make_async_copy(
                src.at[pl.ds(place * lines + chunk * step, step)], dst.at[part(chunk), mine], recv.at[chunk]
            ).start()

    def collect(chunk):
        for j in range(1, group):
            to = lax.rem(place + j, group)
            remote(
                wgt.at[part(chunk), pl.ds(to * planes, planes)],
                out_hbm.at[pl.ds(place * lines + chunk * step, step)],
                send_g, recv_g, device(quarter, to),
            )
        pltpu.make_async_copy(
            wgt.at[part(chunk), pl.ds(place * planes, planes)],
            out_hbm.at[pl.ds(place * lines + chunk * step, step)], recv_g,
        ).start()

    def product(high, low, row, terms, y, base=None):
        total = base
        for col, (x_high, x_low) in terms:
            block = (slice(row * rows, (row + 1) * rows), slice(col * rows, (col + 1) * rows))
            a_high, a_low = high[block], low[block]
            value = dot(a_high, x_high) + (dot(a_high, x_low) + dot(a_low, x_high))
            total = value if total is None else total + value
        return total

    def observe(y, field):
        log_rate = field_scale * field
        observed = res[y]
        intensity = wgt[y] * jnp.exp(log_rate)
        acc[...] += observed * log_rate - intensity
        res[y] = observed - intensity

    def over_lines(chunk, body):
        def at_line(i, carry):
            body(chunk * step + i)
            return carry

        lax.fori_loop(0, step, at_line, 0, unroll=min(step, 2))

    def forward(q, chunk):
        await_bytes(res.at[part(chunk)], recv_c.at[chunk])
        await_bytes(wgt.at[part(chunk)], recv_e.at[chunk])
        if q >= 1:
            await_bytes(f0.at[part(chunk)], recv_f0.at[chunk])
        if q == 2:
            await_bytes(f1.at[part(chunk)], recv_f1.at[chunk])

        def line(y):
            terms = [(q, split(own[y]))]
            if q in (1, 2):
                terms.append((q - 1, split(f0[y])))
            if q == 2:
                terms.append((0, split(f1[y])))
            observe(y, product(lh, ll, q, terms, y, f0[y] if q == 3 else None))
            if q == 2:
                b1[y] = product(lh, ll, 3, terms, y)

        over_lines(chunk, line)
        if q == 2:
            remote(b1.at[part(chunk)], f0.at[part(chunk)], send_z.at[0], recv_f0.at[chunk], device(3, place))
            remote(res.at[part(chunk)], b0.at[part(chunk)], send_z.at[1], recv_b0.at[chunk], device(1, place))
        if q == 3:
            remote(res.at[part(chunk)], b0.at[part(chunk)], send_z.at[0], recv_b0.at[chunk], device(2, place))
            remote(res.at[part(chunk)], b1.at[part(chunk)], send_z.at[1], recv_b1.at[chunk], device(1, place))

    def backward(q, chunk):
        if q <= 2:
            await_bytes(b0.at[part(chunk)], recv_b0.at[chunk])
        if q == 1:
            await_bytes(b1.at[part(chunk)], recv_b1.at[chunk])

        def line(y):
            terms = [(q, split(res[y]))]
            if q in (1, 2):
                terms.append((q + 1, split(b0[y])))
            if q == 1:
                terms.append((3, split(b1[y])))
            wgt[y] = product(th, tl, q, terms, y, b0[y] if q == 0 else None)
            if q == 1:
                f1[y] = product(th, tl, 0, terms, y)

        over_lines(chunk, line)
        if q == 1:
            remote(f1.at[part(chunk)], b0.at[part(chunk)], send_z.at[1], recv_b0.at[chunk], device(0, place))

    def onward(q, chunk):
        await_bytes(own.at[part(chunk)], recv_p.at[chunk])
        if q == 0:
            remote(own.at[part(chunk)], f0.at[part(chunk)], send_z.at[0], recv_f0.at[chunk], device(1, place))
            remote(own.at[part(chunk)], f1.at[part(chunk)], send_z.at[1], recv_f1.at[chunk], device(2, place))
        if q == 1:
            remote(own.at[part(chunk)], f0.at[part(chunk)], send_z.at[0], recv_f0.at[chunk], device(2, place))

    def fetch(chunk):
        return pltpu.make_async_copy(w_hbm.at[pl.ds(chunk * depth, depth)], held, held_sem)

    def square():
        values = held[...]
        prior[...] += jnp.sum((values * values).reshape(depth // 8, 8, values.shape[1]), axis=0)

    def fold(tile):
        return sum(tile[:, k * lanes : (k + 1) * lanes] for k in range(tile.shape[1] // lanes))

    def send_sum_near():
        cells = jnp.sum(acc[...].reshape(rows // 8, 8, acc.shape[1]), axis=0)
        near[place] = fold(cells - 0.5 * prior[...])
        for j in range(1, group):
            remote(near.at[place], near.at[place], send_near, recv_near, device(quarter, lax.rem(place + j, group)))

    def send_sum_far():
        if group > 1:
            others = near.at[pl.ds(0, group - 1)]
            await_bytes(others, send_near)
            await_bytes(others, recv_near)
        far[quarter] = jnp.sum(near[...], axis=0)
        for j in range(1, QUARTERS):
            remote(far.at[quarter], far.at[quarter], send_far, recv_far, device(lax.rem(quarter + j, QUARTERS), place))

    ahead = min(AHEAD, chunks)
    for chunk in range(ahead):
        spread(chunk)

    forward_lag = (1, 1, 1, 2)
    backward_lag = (4, 3, 3, 2)

    def turn(i, carry):
        @pl.when(i < chunks)
        def _():
            fetch(i).start()

        @pl.when(i + ahead < chunks)
        def _():
            spread(i + ahead)

        for q in range(QUARTERS):
            @pl.when((quarter == q) & (i < chunks))
            def _(q=q):
                onward(q, i)

            @pl.when((quarter == q) & (i >= forward_lag[q]) & (i < chunks + forward_lag[q]))
            def _(q=q):
                forward(q, i - forward_lag[q])

            @pl.when((quarter == q) & (i >= backward_lag[q]) & (i < chunks + backward_lag[q]))
            def _(q=q):
                backward(q, i - backward_lag[q])
                collect(i - backward_lag[q])

        @pl.when(i < chunks)
        def _():
            fetch(i).wait()
            square()

        @pl.when(i == chunks + max(forward_lag) - 1)
        def _():
            send_sum_near()

        @pl.when(i == chunks + max(forward_lag))
        def _():
            send_sum_far()

        return carry

    lax.fori_loop(0, chunks + max(backward_lag), turn, 0)

    others = far.at[pl.ds(0, QUARTERS - 1)]
    await_bytes(others, send_far)
    await_bytes(others, recv_far)
    density[...] = jnp.sum(far[...], axis=0)

    away = pl.ds(0, (group - 1) * lines)
    if group > 1:
        for k, src in enumerate((q_hbm, cnt_hbm, exp_hbm)):
            await_bytes(src.at[away], send_in.at[k])
        await_bytes(out_hbm.at[away], send_g)
    for k in range(2):
        await_bytes(own, send_z.at[k])
    await_bytes(out_hbm, recv_g)


def prepare_kernel(w_ref, cnt_ref, exp_ref, th, tl, nh, nl, q_ref, cnt_out, exp_out, held):
    for a in range(w_ref.shape[0]):
        x_high, x_low = split(w_ref[a])
        partly = dot(x_high, th[...]) + (dot(x_low, th[...]) + dot(x_high, tl[...]))
        x_high, x_low = split(partly)
        held[a] = dot(nh[...], x_high) + (dot(nh[...], x_low) + dot(nl[...], x_high))

    def turn(i, carry):
        at = pl.ds(pl.multiple_of(i * 8, 8), 8)
        q_ref[at] = jnp.swapaxes(held[:, at, :], 0, 1)
        cnt_out[at] = jnp.swapaxes(cnt_ref[:, at, :].astype(jnp.float32), 0, 1)
        exp_out[at] = jnp.swapaxes(exp_ref[:, at, :].astype(jnp.float32), 0, 1)
        return carry

    lax.fori_loop(0, w_ref.shape[1] // 8, turn, 0, unroll=2)


def prepare(whitened, counts, exposure, north, time):
    planes, lines, times = whitened.shape
    block = 8
    taken = pl.BlockSpec((block, lines, times), lambda i: (i, 0, 0))
    given = pl.BlockSpec((lines, block, times), lambda i: (0, i, 0))
    fixed = [pl.BlockSpec((extent, extent), lambda i: (0, 0)) for extent in (times, times, lines, lines)]
    return pl.pallas_call(
        prepare_kernel,
        grid=(planes // block,),
        out_shape=[jax.ShapeDtypeStruct((lines, planes, times), jnp.float32)] * 3,
        in_specs=[taken] * 3 + fixed,
        out_specs=[given] * 3,
        scratch_shapes=[pltpu.VMEM((block, lines, times), jnp.float32)],
        compiler_params=pltpu.CompilerParams(vmem_limit_bytes=VMEM_BYTES),
    )(whitened, counts, exposure, *halves(time.T), *halves(north))


def exchange(partly, counts, exposure, whitened, east, group):
    lines = partly.shape[0] // group
    rows = partly.shape[1] * group
    times = partly.shape[2]
    chunks = min(MAX_CHUNKS, lines)
    high, low = halves(east)
    depth = whitened.shape[0] // chunks
    whole = lambda: pltpu.VMEM((lines, rows, times), jnp.float32)
    any_space = pl.BlockSpec(memory_space=pl.ANY)
    in_vmem = pl.BlockSpec(memory_space=pltpu.VMEM)
    dma = pltpu.SemaphoreType.DMA
    return pl.pallas_call(
        functools.partial(kernel, group, chunks),
        out_shape=(
            jax.ShapeDtypeStruct(partly.shape, jnp.float32),
            jax.ShapeDtypeStruct((8, 128), jnp.float32),
        ),
        in_specs=[any_space] * 4 + [in_vmem] * 4,
        out_specs=(any_space, in_vmem),
        scratch_shapes=[whole() for _ in range(7)]
        + [
            pltpu.VMEM((rows, times), jnp.float32),
            pltpu.VMEM((8, times), jnp.float32),
            pltpu.VMEM((depth, times), jnp.float32),
            pltpu.VMEM((group, 8, 128), jnp.float32),
            pltpu.VMEM((QUARTERS, 8, 128), jnp.float32),
        ]
        + [dma((3,))]
        + [dma((chunks,)) for _ in range(3)]
        + [dma((2,))]
        + [dma((chunks,)) for _ in range(4)]
        + [dma] * 7,
        compiler_params=pltpu.CompilerParams(
            collective_id=0, has_side_effects=True, vmem_limit_bytes=VMEM_BYTES
        ),
    )(partly, counts, exposure, whitened, high, low, high.T, low.T)


def per_device(whitened, counts, exposure, cholesky_east, cholesky_north, cholesky_time):
    slabs = lax.axis_size("slab")
    cell_count = whitened.shape[0] * whitened.shape[1] * whitened.shape[2]
    partly, counts_lines, exposure_lines = prepare(whitened, counts, exposure, cholesky_north, cholesky_time)
    flat = jnp.reshape(whitened, (-1, whitened.shape[2]))
    adjoint, terms = exchange(partly, counts_lines, exposure_lines, flat, cholesky_east, slabs // QUARTERS)
    adjoint = jnp.einsum("yat,yb->abt", adjoint, cholesky_north, precision=HIGH)
    adjoint = jnp.einsum("abt,tc->abc", adjoint, cholesky_time, precision=HIGH)
    gradient = field_scale * adjoint - whitened
    density = jnp.sum(terms) / (cell_count * slabs)
    return (gradient, jnp.reshape(density, (1,)))


def solution(mesh):
    placed = (
        P(("chain", "slab"), None, None),
        P(("chain", "slab"), None, None),
        P(("chain", "slab"), None, None),
        P(),
        P(),
        P(),
    )
    return jax.shard_map(
        per_device,
        mesh=mesh,
        in_specs=placed,
        out_specs=(P(("chain", "slab"), None, None), P("chain")),
        check_vma=False,
    )
```
